32 devices in a mesh: groups: 2 (over y), cell: 4 (over z), member: 4 (over x, core).
Axes of the slice: x: 2, y: 2, z: 4, core: 2. Of those that a mesh axis runs over, the one named last changes fastest.
Arguments:
- prior_sample_set: float32 [512, 3, 32, 512], P(('groups', 'member'), None, 'cell'), parts along dimension 0, may hold values from -6 to 6
- wind_table: float32 [8, 2], replicated, may hold values from -0.45 to 0.45
- regimes: int32 [16, 4], P('groups'), parts along dimension 0, may hold values from 0 to 7
- obs_index: int32 [8, 512], P(('groups', 'cell')), parts along dimension 0, may hold values from 0 to 4095
- obs_count: int32 [8], P(('groups', 'cell')), parts along dimension 0, may hold values from 1 to 512, as said below
- obs_value: float32 [8, 512], P(('groups', 'cell')), parts along dimension 0, may hold values from -6 to 6
- obs_var: float32 [8, 512], P(('groups', 'cell')), parts along dimension 0, may hold values from 0.25 to 4
Outputs:
- posterior_sample_set: float32 [512, 3, 32, 512], P(('groups', 'member'), None, 'cell'), parts along dimension 0
The draws below stay inside these ranges and needn't reach their ends.
There are 2 independent parts, one for each index of `groups`. The reference program is written for one: setup_inputs(seed, part) draws one part's arguments, and reference() takes and returns one part's arrays. A program takes and returns all parts, laid end to end along the dimension named above; an argument that names none is the same for every part. Nothing has to cross between parts.
Inputs may be any that keep to these rules, and one draw needn't show every extreme that they name: `obs_count`: some tile has exactly 512 live slots.
All inputs are finite; a program needn't handle non-finite values.
Results may differ from the reference program's by a relative error of at most 0.019.
The reference program's roundings to bfloat16 on the way count: a program that leaves them out, or rounds other values in their place, can miss the bound.
Values may be sent and summed in bfloat16 or wider, within the bound.
A program may use at most 64 MiB of HBM per device.

```python
import math
import jax
import jax.numpy as jnp
from jax import lax

REALIZATION_NUM = 256
FIELDS = 3
MESH_WIDTH = 512
PATCH_HEIGHT = 8
SUBSTEPS = 4
BAND = 4
REGIMES = 8
OBS_T = 512
ROOT_STEPS = 24
NX = 32
N_CELL = 4


def draw_obs_count(key, part):
    counts = jax.random.randint(jax.random.fold_in(key, 11), (N_CELL,), 1, OBS_T + 1)
    full_tile = jax.random.randint(jax.random.fold_in(key, 12), (), 0, N_CELL)
    return jnp.where(jnp.arange(N_CELL) == full_tile, OBS_T, counts).astype(jnp.int32)


def draw_prior_sample_set(key, part):
    shape_full = (REALIZATION_NUM, FIELDS, NX, MESH_WIDTH)
    noise = jax.random.normal(jax.random.fold_in(key, 21), shape_full, jnp.float32)
    offset = 2.0 * jax.random.normal(jax.random.fold_in(key, 22), (REALIZATION_NUM, 1, 1, 1), jnp.float32)
    return jnp.clip(noise + offset, -6.0, 6.0).astype(jnp.float32)


def touch_ends(array, stream_key, smallest, high):
    shape = array.shape
    spot = [jax.random.randint(jax.random.fold_in(stream_key, axis), (), 0, shape[axis]) for axis in range(len(shape))]
    array = array.at[tuple(spot)].set(smallest)
    longest = shape.index(max(shape))
    spot[longest] = (spot[longest] + 1) % shape[longest]
    return array.at[tuple(spot)].set(high)


def steps_of(stream_key, shape, split, low, largest):
    def one(axis_at, blocks):
        steps = jax.random.uniform(jax.random.fold_in(jax.random.fold_in(stream_key, 6), axis_at), (blocks,), jnp.float32, low / len(split), largest / len(split))
        return jnp.repeat(jnp.exp(steps), shape[axis_at] // blocks).reshape((-1,) + (1,) * (len(shape) - axis_at - 1))

    loudness = one(*split[0])
    for cut in split[1:]:
        loudness = loudness * one(*cut)
    return loudness


def gaussian(key, extent, scale, reach, shards=(), kind=jnp.bfloat16):
    values = jax.random.normal(key, extent, jnp.float32) * scale
    if len(shards) > 0:
        values = steps_of(key, extent, shards, -0.22, 0.18) * values
    return jnp.clip(values, min=-reach, max=reach).astype(kind)


def setup_inputs(seed: int = 0, part: int = 0) -> dict:
    seeds = jax.random.split(jax.random.key(seed), 8)
    own_keys = jax.random.split(jax.random.fold_in(seeds[7], part), 8)
    prior_sample_set = draw_prior_sample_set(jax.random.fold_in(jax.random.fold_in(seeds[7], part), 71), part)
    wind_table = jnp.clip(jax.random.uniform(seeds[1], (REGIMES, 2), jnp.float32, -0.45, 0.45), -0.45, 0.45)
    regimes = touch_ends(jax.random.randint(own_keys[2], (NX // BAND, SUBSTEPS), 0, REGIMES), jax.random.fold_in(own_keys[2], 1), 0, REGIMES - 1).astype(jnp.int32)
    obs_index = touch_ends(jax.random.randint(own_keys[3], (N_CELL, OBS_T), 0, PATCH_HEIGHT * MESH_WIDTH), jax.random.fold_in(own_keys[3], 1), 0, (PATCH_HEIGHT * MESH_WIDTH) - 1).astype(jnp.int32)
    obs_count = draw_obs_count(jax.random.fold_in(jax.random.fold_in(seeds[7], part), 71), part)
    obs_value = gaussian(own_keys[5], (N_CELL, OBS_T), 1.0, 6.0, ((0, 4),), jnp.float32)
    obs_var = jnp.clip(jnp.exp(math.log(4.0) - 2.7725887 * jax.random.uniform(own_keys[6], (N_CELL, OBS_T), jnp.float32) ** steps_of(own_keys[6], (N_CELL, OBS_T), ((0, 4),), -0.2, 0.2)), 0.25, 4.0)
    return dict(prior_sample_set=prior_sample_set, wind_table=wind_table, regimes=regimes, obs_index=obs_index, obs_count=obs_count, obs_value=obs_value, obs_var=obs_var)


diffusion = 0.02

def row_speeds(row_ids, regime_column, wind_table, row_total):
    band_ids = jnp.clip(row_ids, 0, row_total - 1) // BAND
    band_hits = (band_ids[:, None] == jnp.arange(regime_column.shape[0])[None, :]).astype(jnp.int32)
    regime_ids = lax.optimization_barrier(jnp.sum(band_hits * regime_column[None, :], axis=1))
    regime_hits = (regime_ids[:, None] == jnp.arange(wind_table.shape[0])[None, :]).astype(jnp.float32)
    speed = jnp.dot(regime_hits, wind_table, precision=lax.Precision.HIGHEST, preferred_element_type=jnp.float32)
    return (speed[:, 0:1], speed[:, 1:2])

def stencil(padded, speed_x, speed_y):
    centre = padded[..., 1:-1, :]
    south = padded[..., :-2, :]
    north = padded[..., 2:, :]
    widths = [(0, 0)] * (centre.ndim - 1) + [(1, 1)]
    sides = jnp.pad(centre, widths)
    west = sides[..., :-2]
    east = sides[..., 2:]
    result = centre - jnp.maximum(speed_x, 0.0) * (centre - south) - jnp.minimum(speed_x, 0.0) * (north - centre)
    result = result - jnp.maximum(speed_y, 0.0) * (centre - west) - jnp.minimum(speed_y, 0.0) * (east - centre)
    return result + diffusion * (north + south + east + west - 4.0 * centre)

def inverse_root(precision_matrix):
    size_n = precision_matrix.shape[0]
    identity = jnp.eye(size_n, dtype=jnp.float32)
    scale = jnp.trace(precision_matrix)
    start = (precision_matrix / scale, identity)

    def newton_step(index, carry):
        upper, lower = carry
        middle = 1.5 * identity - 0.5 * jnp.dot(lower, upper, precision=lax.Precision.HIGHEST, preferred_element_type=jnp.float32)
        upper = jnp.dot(upper, middle, precision=lax.Precision.HIGHEST, preferred_element_type=jnp.float32)
        lower = jnp.dot(middle, lower, precision=lax.Precision.HIGHEST, preferred_element_type=jnp.float32)
        return (upper, lower)
    upper, lower = lax.fori_loop(0, ROOT_STEPS, newton_step, start)
    return (lower, scale)

def analysis(gram, gain, members):
    identity = jnp.eye(members, dtype=jnp.float32)
    precision_matrix = gram + (members - 1.0) * identity
    root_inverse, scale = inverse_root(precision_matrix)
    half_way = jnp.dot(root_inverse, gain, precision=lax.Precision.HIGHEST, preferred_element_type=jnp.float32)
    mean_weights = jnp.dot(root_inverse, half_way, precision=lax.Precision.HIGHEST, preferred_element_type=jnp.float32) / scale
    root = jnp.sqrt((members - 1.0) / scale) * root_inverse
    blend = mean_weights[:, None] + root
    transform = blend - lax.optimization_barrier(jnp.mean(blend, axis=0, keepdims=True)) + 1.0 / members
    return transform.astype(jnp.bfloat16)

def reference(prior_sample_set, wind_table, regimes, obs_index, obs_count, obs_value, obs_var):
    row_ids = jnp.arange(NX)
    speeds = [row_speeds(row_ids, regimes[:, step], wind_table, NX) for step in range(SUBSTEPS)]

    def predict_one_realization(realization_values):
        sample_set_values = realization_values
        for step in range(SUBSTEPS):
            padded = jnp.pad(sample_set_values, ((0, 0), (1, 1), (0, 0)))
            sample_set_values = stencil(padded, speeds[step][0], speeds[step][1])
        return sample_set_values
    predicted_values = lax.map(predict_one_realization, prior_sample_set)
    predicted_reduced_precise = predicted_values.astype(jnp.bfloat16)
    first_cloud_cover = predicted_values[:, 0].reshape(REALIZATION_NUM, N_CELL, PATCH_HEIGHT * MESH_WIDTH)
    predicted = first_cloud_cover[:, jnp.arange(N_CELL)[:, None], obs_index].reshape(REALIZATION_NUM, N_CELL * OBS_T)
    ybar = lax.optimization_barrier(jnp.mean(predicted, axis=0))
    spread = predicted - ybar[None, :]
    live = (jnp.arange(OBS_T)[None, :] < obs_count[:, None]).astype(jnp.float32)
    weight = (live / jnp.sqrt(obs_var)).reshape(-1)
    scaled = spread * weight[None, :]
    gram = jnp.dot(scaled, scaled.T, precision=lax.Precision.HIGHEST, preferred_element_type=jnp.float32)
    innovation = weight * (obs_value.reshape(-1) - ybar)
    gain = jnp.dot(scaled, innovation, precision=lax.Precision.HIGHEST, preferred_element_type=jnp.float32)
    update_matrix_reduced_precise = analysis(gram, gain, REALIZATION_NUM)
    posterior_sample_set = jnp.dot(update_matrix_reduced_precise.T, predicted_reduced_precise.reshape(REALIZATION_NUM, -1), preferred_element_type=jnp.float32)
    return posterior_sample_set.reshape(REALIZATION_NUM, FIELDS, NX, MESH_WIDTH)
```

```python
import functools
import math

import jax
import jax.numpy as jnp
from jax import lax
from jax.experimental import pallas as pl
from jax.experimental.pallas import tpu as pltpu
from jax.sharding import PartitionSpec as P

SUBSTEPS = 4
BAND = 4
ROOT_STEPS = 24
HALO = SUBSTEPS
DIFFUSION = 0.02
MESH = pl.DeviceIdType.MESH
HIGHEST = lax.Precision.HIGHEST
VMEM_LIMIT = 40 * 1024 * 1024
CHUNK = 16
ROWS_SENT = 1
EARLY = 2
LATE_FIRST = 1
LATE_SECOND = 3
LANES = 128
VALUE_TOP = 6.0
VAR_LEAST = 0.25


def split3(x):
    high = x.astype(jnp.bfloat16)
    rest = x - high.astype(jnp.float32)
    middle = rest.astype(jnp.bfloat16)
    return high, middle, (rest - middle.astype(jnp.float32)).astype(jnp.bfloat16)


def six_products(a, b):
    left = jnp.concatenate([a[2], a[1], a[0], a[1], a[0], a[0]], axis=1)
    right = jnp.concatenate([b[0], b[1], b[2], b[0], b[1], b[0]], axis=0)
    return jnp.dot(left, right, preferred_element_type=jnp.float32)


def nt_dot(a, b):
    return lax.dot_general(
        a, b, (((1,), (1,)), ((), ())), precision=HIGHEST, preferred_element_type=jnp.float32
    )


def nn_dot(a, b):
    return jnp.dot(a, b, precision=HIGHEST, preferred_element_type=jnp.float32)


def split1(x):
    return (x.astype(jnp.bfloat16),)


def split2(x):
    high = x.astype(jnp.bfloat16)
    return high, (x - high.astype(jnp.float32)).astype(jnp.bfloat16)


def one_product(a, b):
    return jnp.dot(a[0], b[0], preferred_element_type=jnp.float32)


def three_products(a, b):
    left = jnp.concatenate([a[1], a[0], a[0]], axis=1)
    right = jnp.concatenate([b[0], b[1], b[0]], axis=0)
    return jnp.dot(left, right, preferred_element_type=jnp.float32)


def six_in_halves(a, b):
    middle = a[0].shape[0] // 2
    top = six_products([x[:middle] for x in a], b)
    return jnp.concatenate([top, six_products([x[middle:] for x in a], b)], axis=0)


def phase_ends(members, slots):
    trace = (members - 1) * members + VALUE_TOP**2 / VAR_LEAST * members * slots
    smallest = (members - 1) / trace

    def steps_to(level):
        return min(ROOT_STEPS, max(0, math.ceil(math.log(level / smallest) / math.log(2.25))))

    return steps_to(1e-4), steps_to(0.25)


def cycle_kernel(
    n_cell,
    n_member,
    regime_ref,
    wind_ref,
    count_ref,
    index_ref,
    value_ref,
    var_ref,
    x_hbm,
    out_ref,
    table,
    field_in,
    hits,
    keep,
    edge_up,
    edge_down,
    south,
    north,
    pieces,
    coeff,
    everyone,
    scaled,
    mine,
    others,
    gains,
    gram,
    upper,
    lower,
    read_sem,
    send_up,
    recv_up,
    send_down,
    recv_down,
    send_pred,
    recv_pred,
    send_pass,
    recv_pass,
    send_part,
    recv_part,
    send_gain,
    recv_gain,
    send_sum,
    recv_sum,
    send_pair,
    recv_pair,
    send_far,
    recv_far,
    send_mate,
    recv_mate,
):
    cell = lax.axis_index("cell")
    member = lax.axis_index("member")
    fields, rows, count, width = field_in.shape
    slots = index_ref.shape[1]
    members = count * n_member
    chips = n_member // 2
    parity = lax.rem(member, 2)
    mate = member + 1 - 2 * parity
    half = members // 2
    part = half // n_cell
    chunks = count // CHUNK
    has_south, has_north = cell > 0, cell < n_cell - 1

    def block_of(owner):
        return pl.ds(pl.multiple_of(owner * count, count), count)

    own = block_of(member)

    def read_row(f, r):
        return pltpu.make_async_copy(x_hbm.at[:, f, r, :], field_in.at[f, r], read_sem.at[f, r])

    for f in range(fields):
        for r in range(rows):
            read_row(f, r).start()

    barrier = pltpu.get_barrier_semaphore()
    for d in range(1, chips):
        pl.semaphore_signal(
            barrier, inc=1, device_id={"member": lax.rem(member + 2 * d, n_member)}, device_id_type=MESH
        )
    pl.semaphore_signal(barrier, inc=1, device_id={"member": mate}, device_id_type=MESH)
    for d in range(1, n_cell):
        pl.semaphore_signal(
            barrier, inc=1, device_id={"cell": lax.rem(cell + d, n_cell)}, device_id_type=MESH
        )

    def remote(src, dst, send, recv, **device):
        return pltpu.make_async_remote_copy(
            src_ref=src,
            dst_ref=dst,
            send_sem=send,
            recv_sem=recv,
            device_id=device,
            device_id_type=MESH,
        )

    above = lax.rem(cell + 1, n_cell)
    below = lax.rem(cell + n_cell - 1, n_cell)

    def upward(f, c):
        at, u = pl.ds(c * CHUNK, CHUNK), f * chunks + c
        return remote(
            edge_up.at[f, :, at], south.at[f, :, at], send_up.at[u], recv_up.at[u], cell=above
        )

    def downward(f, c):
        at, u = pl.ds(c * CHUNK, CHUNK), f * chunks + c
        return remote(
            edge_down.at[f, :, at], north.at[f, :, at], send_down.at[u], recv_down.at[u], cell=below
        )

    def send_edges(f, c):
        at = pl.ds(c * CHUNK, CHUNK)
        for i in range(HALO):
            edge_up[f, i, at, :] = field_in[f, rows - HALO + i, at, :].astype(jnp.bfloat16)
            edge_down[f, i, at, :] = field_in[f, i, at, :].astype(jnp.bfloat16)

        @pl.when(has_north)
        def _():
            upward(f, c).start()

        @pl.when(has_south)
        def _():
            downward(f, c).start()

    def wait_edges(f, c):
        @pl.when(has_south)
        def _():
            upward(f, c).wait_recv()

        @pl.when(has_north)
        def _():
            downward(f, c).wait_recv()

    whole_field = [(0, pl.ds(0, rows), pl.ds(c * CHUNK, CHUNK)) for c in range(chunks)]
    row_groups = [
        [(f, pl.ds(g, ROWS_SENT), pl.ds(0, count)) for g in range(0, rows, ROWS_SENT)]
        for f in range(1, fields)
    ]
    units = whole_field + [unit for group in row_groups for unit in group]
    units_of = [list(range(chunks))]
    for group in row_groups:
        first = units_of[-1][-1] + 1
        units_of.append(list(range(first, first + len(group))))

    def unit_ref(owner, u):
        f, r, m = units[u]
        return pieces.at[owner, f, r, m]

    def to_far(d, u):
        here = unit_ref(member, u)
        peer = lax.rem(member + 2 * d, n_member)
        return remote(here, here, send_far.at[d, u], recv_far.at[d, u], member=peer)

    def to_mate(d, u):
        there = unit_ref(lax.rem(member + n_member - 2 * d, n_member), u)
        return remote(there, there, send_mate.at[d, u], recv_mate.at[d, u], member=mate)

    def send_far_unit(u):
        for d in range(1, chips):
            to_far(d, u).start()

    def forward_unit(u):
        for d in range(1, chips):
            to_far(d, u).wait_recv()
            to_mate(d, u).start()

    row_total = rows * n_cell

    def one_table_row(i, carry):
        row = cell * rows + i - HALO
        inside = jnp.where((row >= 0) & (row < row_total), 1.0, 0.0)
        band = jnp.minimum(jnp.maximum(row, 0), row_total - 1) // BAND
        for s in range(SUBSTEPS):
            regime = regime_ref[s, band]
            cx, cy = wind_ref[0, regime], wind_ref[1, regime]
            x_up, x_down = jnp.maximum(cx, 0.0), jnp.minimum(cx, 0.0)
            y_up, y_down = jnp.maximum(cy, 0.0), jnp.minimum(cy, 0.0)
            table[s * 5, i] = inside * (1.0 - 4.0 * DIFFUSION - x_up + x_down - y_up + y_down)
            table[s * 5 + 1, i] = inside * (x_up + DIFFUSION)
            table[s * 5 + 2, i] = inside * (DIFFUSION - x_down)
            table[s * 5 + 3, i] = inside * (y_up + DIFFUSION)
            table[s * 5 + 4, i] = inside * (DIFFUSION - y_down)
        return carry

    for r in range(rows):
        read_row(0, r).wait()
    pl.semaphore_wait(barrier, chips + n_cell - 1)
    for c in range(chunks):
        send_edges(0, c)
    lax.fori_loop(0, rows + 2 * HALO, one_table_row, 0)

    @pl.when(cell == 0)
    def _():
        south[...] = jnp.zeros_like(south)

    @pl.when(cell == n_cell - 1)
    def _():
        north[...] = jnp.zeros_like(north)

    late_edges = [(f, c) for f in range(2, fields) for c in range(chunks)]
    for f in range(1, fields):
        for r in range(rows):
            read_row(f, r).wait()
    for c in range(chunks):
        send_edges(1, c)
    for f, c in late_edges[:LATE_FIRST]:
        send_edges(f, c)

    column = lax.broadcasted_iota(jnp.int32, (width, slots), 0)

    def mark_row(i, carry):
        hit = jnp.where(column == index_ref[...] - i * width, 1.0, 0.0)
        hits[i] = hit.astype(jnp.bfloat16)
        return carry

    lax.fori_loop(0, rows, mark_row, 0)

    lane = lax.broadcasted_iota(jnp.int32, (CHUNK, LANES), 1)

    def west_of(q):
        moved = pltpu.roll(q, 1, 1)
        first = jnp.where(lane == 0, 0.0, moved[:, :LANES])
        return jnp.concatenate([first, moved[:, LANES:]], axis=1)

    def east_of(q):
        moved = pltpu.roll(q, width - 1, 1)
        last = jnp.where(lane == LANES - 1, 0.0, moved[:, width - LANES :])
        return jnp.concatenate([moved[:, : width - LANES], last], axis=1)

    def stencil_chunk(f, c):
        at = pl.ds(pl.multiple_of(c * CHUNK, CHUNK), CHUNK)
        cells = [south[f, i, at, :].astype(jnp.float32) for i in range(HALO)]
        cells += [field_in[f, i, at, :] for i in range(rows)]
        cells += [north[f, i, at, :].astype(jnp.float32) for i in range(HALO)]
        for s in range(SUBSTEPS):
            fresh = list(cells)
            for i in range(s + 1, rows + 2 * HALO - s - 1):
                q = cells[i]
                fresh[i] = (
                    q * table[s * 5, i]
                    + cells[i - 1] * table[s * 5 + 1, i]
                    + cells[i + 1] * table[s * 5 + 2, i]
                    + west_of(q) * table[s * 5 + 3, i]
                    + east_of(q) * table[s * 5 + 4, i]
                )
            cells = fresh
        for i in range(rows):
            pieces[member, f, i, at, :] = cells[HALO + i].astype(jnp.bfloat16)
            if isinstance(f, int) and f == 0:
                keep[i, at, :] = cells[HALO + i]

    def stencil_field(f):
        for c in range(chunks):
            wait_edges(f, c)

        def one_chunk(c, carry):
            stencil_chunk(f, c)
            return carry

        lax.fori_loop(0, chunks, one_chunk, 0)

    for c in range(chunks):
        wait_edges(0, c)
        stencil_chunk(0, c)
        if c < EARLY:
            send_far_unit(c)

    highs, lows = [], []
    for i in range(rows):
        high = keep[i].astype(jnp.bfloat16)
        highs.append(high)
        lows.append((keep[i] - high.astype(jnp.float32)).astype(jnp.bfloat16))
    source = jnp.concatenate(
        [jnp.concatenate(highs, axis=1), jnp.concatenate(lows, axis=1)], axis=0
    )
    width2 = slots // 2
    for side in range(2):
        at = pl.ds(side * width2, width2)
        target = hits[:, :, at].reshape(rows * width, width2)
        picked = jnp.dot(source, target, preferred_element_type=jnp.float32)
        everyone[own, at] = picked[:count] + picked[count:]

    def share_pred(d):
        peer = lax.rem(member + 2 * d, n_member)
        return remote(
            everyone.at[own], everyone.at[own], send_pred.at[d], recv_pred.at[d], member=peer
        )

    def pass_pred(d):
        at = block_of(lax.rem(member + n_member - 2 * d, n_member))
        return remote(
            everyone.at[at], everyone.at[at], send_pass.at[d], recv_pass.at[d], member=mate
        )

    for d in range(1, chips):
        share_pred(d).start()
    pass_pred(0).start()
    for c in range(EARLY, chunks):
        send_far_unit(c)
    stencil_field(1)
    for u in units_of[1]:
        send_far_unit(u)
    for d in range(1, chips):
        share_pred(d).wait_recv()
        pass_pred(d).start()
    for d in range(chips):
        pass_pred(d).wait_recv()

    predicted = everyone[...]
    ybar = jnp.mean(predicted, axis=0, keepdims=True)
    live = lax.broadcasted_iota(jnp.int32, (1, slots), 1) < count_ref[0]
    weight = jnp.where(live, 1.0, 0.0) / jnp.sqrt(var_ref[...])
    scaled[...] = (predicted - ybar) * weight
    innovation = jnp.broadcast_to(weight * (value_ref[...] - ybar), (8, slots))
    local = scaled[pl.ds(pl.multiple_of(parity * half, half), half), :]
    product = nt_dot(jnp.concatenate([local, innovation], axis=0), scaled[...])
    mine[...] = product[:half]
    gains[0] = product[half : half + 1]

    def part_of(q):
        return pl.ds(pl.multiple_of(q * part, part), part)

    def share_part(d):
        peer = lax.rem(cell + d, n_cell)
        return remote(
            mine.at[part_of(peer)], others.at[d - 1], send_part.at[d], recv_part.at[d], cell=peer
        )

    def share_gain(d):
        peer = lax.rem(cell + d, n_cell)
        return remote(gains.at[0], gains.at[d], send_gain.at[d], recv_gain.at[d], cell=peer)

    def sum_of(q):
        return pl.ds(pl.multiple_of(parity * half + q * part, part), part)

    def share_sum(d):
        peer = lax.rem(cell + d, n_cell)
        here = gram.at[sum_of(cell)]
        return remote(here, here, send_sum.at[d], recv_sum.at[d], cell=peer)

    def pair_sum(d):
        there = gram.at[sum_of(lax.rem(cell + n_cell - d, n_cell))]
        return remote(there, there, send_pair.at[d], recv_pair.at[d], member=mate)

    for d in range(1, n_cell):
        share_part(d).start()
        share_gain(d).start()
    for f, c in late_edges[LATE_FIRST:LATE_SECOND]:
        send_edges(f, c)
    for f in range(2):
        for u in units_of[f]:
            to_mate(0, u).start()
    for d in range(1, n_cell):
        share_part(d).wait_recv()
    summed = mine[part_of(cell), :]
    for d in range(n_cell - 1):
        summed = summed + others[d]
    gram[sum_of(cell), :] = summed
    for d in range(1, n_cell):
        share_sum(d).start()
    pair_sum(0).start()
    for f, c in late_edges[LATE_SECOND:]:
        send_edges(f, c)
    for f, c in late_edges[:LATE_SECOND]:
        wait_edges(f, c)
        stencil_chunk(f, c)
    for d in range(1, n_cell):
        share_sum(d).wait_recv()
        pair_sum(d).start()
    for f, c in late_edges[LATE_SECOND:]:
        wait_edges(f, c)
        stencil_chunk(f, c)
    for f in range(2, fields):
        for u in units_of[f]:
            send_far_unit(u)
            to_mate(0, u).start()
    for d in range(n_cell):
        pair_sum(d).wait_recv()

    lines = lax.broadcasted_iota(jnp.int32, (members, members), 0)
    columns = lax.broadcasted_iota(jnp.int32, (members, members), 1)
    identity = jnp.where(lines == columns, 1.0, 0.0).astype(jnp.float32)
    precision = gram[...] + (members - 1.0) * identity
    scale = jnp.sum(jnp.sum(precision * identity, axis=1, keepdims=True), axis=0, keepdims=True)
    upper[...] = precision / scale
    lower[...] = identity

    def newton(split, product, powers, of_root):
        def step(at, carry):
            x, z = upper[...], lower[...]
            pieces_of_x = split(x)
            square = product(pieces_of_x, pieces_of_x)
            lower[...] = of_root[0] * z + of_root[1] * three_products(split2(z), split2(x))
            cube = product(split(square), pieces_of_x)
            upper[...] = powers[0] * x + powers[1] * square + powers[2] * cube
            return carry

        return step

    growing, shrinking = (2.25, -1.5, 0.25), (0.0, 0.75, 0.25)
    exact, double = phase_ends(members, slots * n_cell)
    lax.fori_loop(0, exact, newton(split3, six_in_halves, growing, (1.5, -0.5)), 0)
    for u in units_of[0]:
        forward_unit(u)
    lax.fori_loop(exact, double, newton(split2, three_products, growing, (1.5, -0.5)), 0)
    for u in units_of[1]:
        forward_unit(u)
    upper[...] = identity - upper[...]
    lax.fori_loop(double, ROOT_STEPS, newton(split1, one_product, shrinking, (1.0, 0.5)), 0)

    for d in range(1, n_cell):
        share_gain(d).wait_recv()
    gain = gains[0]
    for d in range(1, n_cell):
        gain = gain + gains[d]
    gain = jnp.broadcast_to(gain, (8, members))
    half_way = nt_dot(gain, lower[...])
    mean_weights = nt_dot(half_way, lower[...])[0:1, :] / scale
    root = jnp.sqrt((members - 1.0) / scale) * lower[own, :]
    blend = mean_weights + root
    transform = blend - jnp.mean(blend, axis=1, keepdims=True) + 1.0 / members
    coeff[...] = transform.astype(jnp.bfloat16)

    def arrive(u):
        for d in range(chips):
            to_mate(d, u).wait_recv()

    def blend_row(f, r):
        block = pieces[:, f, r].reshape(members, width)
        out_ref[f, r] = jnp.dot(coeff[...], block, preferred_element_type=jnp.float32)

    for u in units_of[0]:
        arrive(u)

    def blend_loop(r, carry):
        blend_row(0, r)
        return carry

    lax.fori_loop(0, rows, blend_loop, 0)
    for u in units_of[1]:
        arrive(u)

    def blend_loop1(r, carry):
        blend_row(1, r)
        return carry

    lax.fori_loop(0, rows, blend_loop1, 0)
    late = [u for f in range(2, fields) for u in units_of[f]]
    for at, u in enumerate(late):
        forward_unit(u)
        if at > 0:
            finish(arrive, blend_row, units, late[at - 1])
    finish(arrive, blend_row, units, late[-1])

    for f in range(fields):
        for c in range(chunks):

            @pl.when(has_north)
            def _():
                upward(f, c).wait_send()

            @pl.when(has_south)
            def _():
                downward(f, c).wait_send()

    for u in range(len(units)):
        for d in range(1, chips):
            to_far(d, u).wait_send()
        for d in range(chips):
            to_mate(d, u).wait_send()
    for d in range(1, chips):
        share_pred(d).wait_send()
    for d in range(chips):
        pass_pred(d).wait_send()
    for d in range(1, n_cell):
        share_part(d).wait_send()
        share_gain(d).wait_send()
        share_sum(d).wait_send()
    for d in range(n_cell):
        pair_sum(d).wait_send()


def finish(arrive, blend_row, units, u):
    arrive(u)
    f, r, _ = units[u]
    for i in range(r.size):
        blend_row(f, r.start + i)


def write_kernel(blended_ref, out_hbm, sem):
    fields, rows = blended_ref.shape[:2]
    copies = [
        pltpu.make_async_copy(blended_ref.at[f, r], out_hbm.at[:, f, r, :], sem.at[f, r])
        for f in range(fields)
        for r in range(rows)
    ]
    for copy in copies:
        copy.start()
    for copy in copies:
        copy.wait()


def shards(prior_sample_set, wind_table, regimes, obs_index, obs_count, obs_value, obs_var):
    n_cell, n_member = lax.axis_size("cell"), lax.axis_size("member")
    count, fields, rows, width = prior_sample_set.shape
    slots = obs_index.shape[1]
    members = count * n_member
    chips = n_member // 2
    chunks = count // CHUNK
    units = chunks + (fields - 1) * (rows // ROWS_SENT)
    smem = pl.BlockSpec(memory_space=pltpu.SMEM)
    vmem = pl.BlockSpec(memory_space=pltpu.VMEM)
    hbm = pl.BlockSpec(memory_space=pltpu.HBM)
    single, half = jnp.float32, jnp.bfloat16
    edge = pltpu.VMEM((fields, HALO, count, width), half)
    square = pltpu.VMEM((members, members), single)
    part = (members // 2 // n_cell, members)
    dma = pltpu.SemaphoreType.DMA
    prior = pltpu.with_memory_space_constraint(prior_sample_set, pltpu.HBM)
    blended = pl.pallas_call(
        functools.partial(cycle_kernel, n_cell, n_member),
        in_specs=[smem] * 3 + [vmem] * 3 + [hbm],
        out_specs=vmem,
        out_shape=jax.ShapeDtypeStruct((fields, rows, count, width), single),
        scratch_shapes=[
            pltpu.SMEM((SUBSTEPS * 5, rows + 2 * HALO), single),
            pltpu.VMEM((fields, rows, count, width), single),
            pltpu.VMEM((rows, width, slots), half),
            pltpu.VMEM((rows, count, width), single),
            edge,
            edge,
            edge,
            edge,
            pltpu.VMEM((n_member, fields, rows, count, width), half),
            pltpu.VMEM((count, members), half),
            pltpu.VMEM((members, slots), single),
            pltpu.VMEM((members, slots), single),
            pltpu.VMEM((members // 2, members), single),
            pltpu.VMEM((n_cell - 1,) + part, single),
            pltpu.VMEM((n_cell, 1, members), single),
            square,
            square,
            square,
            dma((fields, rows)),
        ]
        + [dma((fields * chunks,))] * 4
        + [dma((chips,))] * 4
        + [dma((n_cell,))] * 8
        + [dma((chips, units))] * 4,
        compiler_params=pltpu.CompilerParams(
            collective_id=0, has_side_effects=True, vmem_limit_bytes=VMEM_LIMIT
        ),
    )(regimes.T, wind_table.T, obs_count, obs_index, obs_value, obs_var, prior)
    return pl.pallas_call(
        write_kernel,
        in_specs=[vmem],
        out_specs=hbm,
        out_shape=jax.ShapeDtypeStruct(prior_sample_set.shape, single),
        scratch_shapes=[dma((fields, rows))],
        compiler_params=pltpu.CompilerParams(vmem_limit_bytes=8 * 1024 * 1024),
    )(blended)


def solution(mesh):
    return jax.shard_map(
        shards,
        mesh=mesh,
        in_specs=(
            P(("groups", "member"), None, "cell", None),
            P(),
            P("groups", None),
            P(("groups", "cell"), None),
            P(("groups", "cell")),
            P(("groups", "cell"), None),
            P(("groups", "cell"), None),
        ),
        out_specs=P(("groups", "member"), None, "cell", None),
        check_vma=False,
    )
```

```python
import functools
import math

import jax
import jax.numpy as jnp
from jax import lax
from jax.experimental import pallas as pl
from jax.experimental.pallas import tpu as pltpu
from jax.sharding import PartitionSpec as P

SUBSTEPS = 4
BAND = 4
ROOT_STEPS = 24
HALO = SUBSTEPS
DIFFUSION = 0.02
MESH = pl.DeviceIdType.MESH
HIGHEST = lax.Precision.HIGHEST
VMEM_LIMIT = 40 * 1024 * 1024
CHUNK = 16
EARLY = 2
LATE_FIRST = 1
LATE_SECOND = 3
LANES = 128
VALUE_TOP = 6.0
VAR_LEAST = 0.25


def split3(x):
    high = x.astype(jnp.bfloat16)
    rest = x - high.astype(jnp.float32)
    middle = rest.astype(jnp.bfloat16)
    return high, middle, (rest - middle.astype(jnp.float32)).astype(jnp.bfloat16)


def six_products(a, b):
    left = jnp.concatenate([a[2], a[1], a[0], a[1], a[0], a[0]], axis=1)
    right = jnp.concatenate([b[0], b[1], b[2], b[0], b[1], b[0]], axis=0)
    return jnp.dot(left, right, preferred_element_type=jnp.float32)


def nt_dot(a, b):
    return lax.dot_general(
        a, b, (((1,), (1,)), ((), ())), precision=HIGHEST, preferred_element_type=jnp.float32
    )


def nn_dot(a, b):
    return jnp.dot(a, b, precision=HIGHEST, preferred_element_type=jnp.float32)


def split1(x):
    return (x.astype(jnp.bfloat16),)


def split2(x):
    high = x.astype(jnp.bfloat16)
    return high, (x - high.astype(jnp.float32)).astype(jnp.bfloat16)


def one_product(a, b):
    return jnp.dot(a[0], b[0], preferred_element_type=jnp.float32)


def three_products(a, b):
    left = jnp.concatenate([a[1], a[0], a[0]], axis=1)
    right = jnp.concatenate([b[0], b[1], b[0]], axis=0)
    return jnp.dot(left, right, preferred_element_type=jnp.float32)


def six_in_halves(a, b):
    middle = a[0].shape[0] // 2
    top = six_products([x[:middle] for x in a], b)
    return jnp.concatenate([top, six_products([x[middle:] for x in a], b)], axis=0)


def phase_ends(members, slots):
    trace = (members - 1) * members + VALUE_TOP**2 / VAR_LEAST * members * slots
    smallest = (members - 1) / trace

    def steps_to(level):
        return min(ROOT_STEPS, max(0, math.ceil(math.log(level / smallest) / math.log(2.25))))

    return steps_to(1e-4), steps_to(0.25)


def cycle_kernel(
    n_cell,
    n_member,
    count_ref,
    regime_hbm,
    wind_hbm,
    index_hbm,
    value_hbm,
    var_hbm,
    x_hbm,
    out_ref,
    regime_ref,
    wind_ref,
    index_ref,
    value_ref,
    var_ref,
    table,
    field_in,
    hits,
    keep,
    edge_up,
    edge_down,
    south,
    north,
    pieces,
    coeff,
    everyone,
    scaled,
    mine,
    others,
    gains,
    gram,
    upper,
    lower,
    read_sem,
    small_sem,
    send_up,
    recv_up,
    send_down,
    recv_down,
    send_pred,
    recv_pred,
    send_pass,
    recv_pass,
    send_part,
    recv_part,
    send_gain,
    recv_gain,
    send_sum,
    recv_sum,
    send_pair,
    recv_pair,
    send_far,
    recv_far,
    send_mate,
    recv_mate,
    send_own,
    recv_own,
):
    cell = lax.axis_index("cell")
    member = lax.axis_index("member")
    fields, rows, count, width = field_in.shape
    slots = index_ref.shape[1]
    members = count * n_member
    chips = n_member // 2
    parity = lax.rem(member, 2)
    mate = member + 1 - 2 * parity
    half = members // 2
    part = half // n_cell
    chunks = count // CHUNK
    has_south, has_north = cell > 0, cell < n_cell - 1

    def block_of(owner):
        return pl.ds(pl.multiple_of(owner * count, count), count)

    own = block_of(member)

    def read_row(f, r):
        return pltpu.make_async_copy(x_hbm.at[:, f, r, :], field_in.at[f, r], read_sem.at[f, r])

    small = [
        pltpu.make_async_copy(source, target, small_sem.at[at])
        for at, (source, target) in enumerate(
            [
                (regime_hbm, regime_ref),
                (wind_hbm, wind_ref),
                (index_hbm, index_ref),
                (value_hbm, value_ref),
                (var_hbm, var_ref),
            ]
        )
    ]
    for r in range(rows):
        read_row(0, r).start()
    for copy in small:
        copy.start()
    for f in range(1, fields):
        for r in range(rows):
            read_row(f, r).start()

    barrier = pltpu.get_barrier_semaphore()
    for d in range(1, chips):
        pl.semaphore_signal(
            barrier, inc=1, device_id={"member": lax.rem(member + 2 * d, n_member)}, device_id_type=MESH
        )
    pl.semaphore_signal(barrier, inc=1, device_id={"member": mate}, device_id_type=MESH)
    for d in range(1, n_cell):
        pl.semaphore_signal(
            barrier, inc=1, device_id={"cell": lax.rem(cell + d, n_cell)}, device_id_type=MESH
        )

    def remote(src, dst, send, recv, **device):
        return pltpu.make_async_remote_copy(
            src_ref=src,
            dst_ref=dst,
            send_sem=send,
            recv_sem=recv,
            device_id=device,
            device_id_type=MESH,
        )

    above = lax.rem(cell + 1, n_cell)
    below = lax.rem(cell + n_cell - 1, n_cell)

    def upward(f, c):
        at, u = pl.ds(c * CHUNK, CHUNK), f * chunks + c
        return remote(
            edge_up.at[f, :, at], south.at[f, :, at], send_up.at[u], recv_up.at[u], cell=above
        )

    def downward(f, c):
        at, u = pl.ds(c * CHUNK, CHUNK), f * chunks + c
        return remote(
            edge_down.at[f, :, at], north.at[f, :, at], send_down.at[u], recv_down.at[u], cell=below
        )

    def send_edges(f, c):
        at = pl.ds(c * CHUNK, CHUNK)
        for i in range(HALO):
            edge_up[f, i, at, :] = field_in[f, rows - HALO + i, at, :].astype(jnp.bfloat16)
            edge_down[f, i, at, :] = field_in[f, i, at, :].astype(jnp.bfloat16)

        @pl.when(has_north)
        def _():
            upward(f, c).start()

        @pl.when(has_south)
        def _():
            downward(f, c).start()

    def wait_edges(f, c):
        @pl.when(has_south)
        def _():
            upward(f, c).wait_recv()

        @pl.when(has_north)
        def _():
            downward(f, c).wait_recv()

    whole_field = [(0, pl.ds(0, rows), pl.ds(c * CHUNK, CHUNK)) for c in range(chunks)]
    row_groups = [
        [(f, pl.ds(start, size), pl.ds(0, count)) for start, size in row_cuts(f, fields, rows)]
        for f in range(1, fields)
    ]
    units = whole_field + [unit for group in row_groups for unit in group]
    units_of = [list(range(chunks))]
    for group in row_groups:
        first = units_of[-1][-1] + 1
        units_of.append(list(range(first, first + len(group))))

    def unit_ref(owner, u):
        f, r, m = units[u]
        return pieces.at[owner, f, r, m]

    def to_far(d, u):
        here = unit_ref(member, u)
        peer = lax.rem(member + 2 * d, n_member)
        return remote(here, here, send_far.at[d, u], recv_far.at[d, u], member=peer)

    def to_mate(d, u):
        there = unit_ref(lax.rem(member + n_member - 2 * d, n_member), u)
        return remote(there, there, send_mate.at[d, u], recv_mate.at[d, u], member=mate)

    def own_to_mate(f):
        here = pieces.at[member, f]
        return remote(here, here, send_own.at[f], recv_own.at[f], member=mate)

    def send_far_unit(u):
        for d in range(1, chips):
            to_far(d, u).start()

    def forward_unit(u):
        for d in range(1, chips):
            to_far(d, u).wait_recv()
            to_mate(d, u).start()

    row_total = rows * n_cell

    def one_table_row(i, carry):
        row = cell * rows + i - HALO
        inside = jnp.where((row >= 0) & (row < row_total), 1.0, 0.0)
        band = jnp.minimum(jnp.maximum(row, 0), row_total - 1) // BAND
        for s in range(SUBSTEPS):
            regime = regime_ref[s, band]
            cx, cy = wind_ref[0, regime], wind_ref[1, regime]
            x_up, x_down = jnp.maximum(cx, 0.0), jnp.minimum(cx, 0.0)
            y_up, y_down = jnp.maximum(cy, 0.0), jnp.minimum(cy, 0.0)
            table[s * 5, i] = inside * (1.0 - 4.0 * DIFFUSION - x_up + x_down - y_up + y_down)
            table[s * 5 + 1, i] = inside * (x_up + DIFFUSION)
            table[s * 5 + 2, i] = inside * (DIFFUSION - x_down)
            table[s * 5 + 3, i] = inside * (y_up + DIFFUSION)
            table[s * 5 + 4, i] = inside * (DIFFUSION - y_down)
        return carry

    for r in range(rows):
        read_row(0, r).wait()
    pl.semaphore_wait(barrier, chips + n_cell - 1)
    for c in range(chunks):
        send_edges(0, c)
    for copy in small:
        copy.wait()
    lax.fori_loop(0, rows + 2 * HALO, one_table_row, 0)

    @pl.when(cell == 0)
    def _():
        south[...] = jnp.zeros_like(south)

    @pl.when(cell == n_cell - 1)
    def _():
        north[...] = jnp.zeros_like(north)

    late_edges = [(f, c) for f in range(2, fields) for c in range(chunks)]
    for f in range(1, fields):
        for r in range(rows):
            read_row(f, r).wait()
    for c in range(chunks):
        send_edges(1, c)
    for f, c in late_edges[:LATE_FIRST]:
        send_edges(f, c)

    column = lax.broadcasted_iota(jnp.int32, (width, slots), 0)

    def mark_row(i, carry):
        hit = jnp.where(column == index_ref[...] - i * width, 1.0, 0.0)
        hits[i] = hit.astype(jnp.bfloat16)
        return carry

    lax.fori_loop(0, rows, mark_row, 0)

    lane = lax.broadcasted_iota(jnp.int32, (CHUNK, LANES), 1)

    def west_of(q):
        moved = pltpu.roll(q, 1, 1)
        first = jnp.where(lane == 0, 0.0, moved[:, :LANES])
        return jnp.concatenate([first, moved[:, LANES:]], axis=1)

    def east_of(q):
        moved = pltpu.roll(q, width - 1, 1)
        last = jnp.where(lane == LANES - 1, 0.0, moved[:, width - LANES :])
        return jnp.concatenate([moved[:, : width - LANES], last], axis=1)

    def stencil_chunk(f, c):
        at = pl.ds(pl.multiple_of(c * CHUNK, CHUNK), CHUNK)
        cells = [south[f, i, at, :].astype(jnp.float32) for i in range(HALO)]
        cells += [field_in[f, i, at, :] for i in range(rows)]
        cells += [north[f, i, at, :].astype(jnp.float32) for i in range(HALO)]
        for s in range(SUBSTEPS):
            fresh = list(cells)
            for i in range(s + 1, rows + 2 * HALO - s - 1):
                q = cells[i]
                fresh[i] = (
                    q * table[s * 5, i]
                    + cells[i - 1] * table[s * 5 + 1, i]
                    + cells[i + 1] * table[s * 5 + 2, i]
                    + west_of(q) * table[s * 5 + 3, i]
                    + east_of(q) * table[s * 5 + 4, i]
                )
            cells = fresh
        for i in range(rows):
            pieces[member, f, i, at, :] = cells[HALO + i].astype(jnp.bfloat16)
            if isinstance(f, int) and f == 0:
                keep[i, at, :] = cells[HALO + i]

    for c in range(chunks):
        wait_edges(0, c)
        stencil_chunk(0, c)
        if c < EARLY:
            send_far_unit(c)

    highs, lows = [], []
    for i in range(rows):
        high = keep[i].astype(jnp.bfloat16)
        highs.append(high)
        lows.append((keep[i] - high.astype(jnp.float32)).astype(jnp.bfloat16))
    source = jnp.concatenate(
        [jnp.concatenate(highs, axis=1), jnp.concatenate(lows, axis=1)], axis=0
    )
    width2 = slots // 2
    for side in range(2):
        at = pl.ds(side * width2, width2)
        target = hits[:, :, at].reshape(rows * width, width2)
        picked = jnp.dot(source, target, preferred_element_type=jnp.float32)
        everyone[own, at] = picked[:count] + picked[count:]

    def share_pred(d):
        peer = lax.rem(member + 2 * d, n_member)
        return remote(
            everyone.at[own], everyone.at[own], send_pred.at[d], recv_pred.at[d], member=peer
        )

    def pass_pred(d):
        at = block_of(lax.rem(member + n_member - 2 * d, n_member))
        return remote(
            everyone.at[at], everyone.at[at], send_pass.at[d], recv_pass.at[d], member=mate
        )

    for d in range(1, chips):
        share_pred(d).start()
    pass_pred(0).start()
    for c in range(EARLY, chunks):
        send_far_unit(c)
    for c in range(chunks):
        if c == chunks - 1:
            for d in range(1, chips):
                share_pred(d).wait_recv()
                pass_pred(d).start()
        wait_edges(1, c)
        stencil_chunk(1, c)
    for u in units_of[1]:
        send_far_unit(u)
    for d in range(chips):
        pass_pred(d).wait_recv()

    predicted = everyone[...]
    ybar = jnp.mean(predicted, axis=0, keepdims=True)
    live = lax.broadcasted_iota(jnp.int32, (1, slots), 1) < count_ref[0]
    weight = jnp.where(live, 1.0, 0.0) / jnp.sqrt(var_ref[...])
    scaled[...] = (predicted - ybar) * weight
    innovation = jnp.broadcast_to(weight * (value_ref[...] - ybar), (8, slots))
    local = scaled[pl.ds(pl.multiple_of(parity * half, half), half), :]
    product = nt_dot(jnp.concatenate([local, innovation], axis=0), scaled[...])
    mine[...] = product[:half]
    gains[0] = product[half : half + 1]

    def part_of(q):
        return pl.ds(pl.multiple_of(q * part, part), part)

    def share_part(d):
        peer = lax.rem(cell + d, n_cell)
        return remote(
            mine.at[part_of(peer)], others.at[d - 1], send_part.at[d], recv_part.at[d], cell=peer
        )

    def share_gain(d):
        peer = lax.rem(cell + d, n_cell)
        return remote(gains.at[0], gains.at[d], send_gain.at[d], recv_gain.at[d], cell=peer)

    def sum_of(q):
        return pl.ds(pl.multiple_of(parity * half + q * part, part), part)

    def share_sum(d):
        peer = lax.rem(cell + d, n_cell)
        here = gram.at[sum_of(cell)]
        return remote(here, here, send_sum.at[d], recv_sum.at[d], cell=peer)

    def pair_sum(d):
        there = gram.at[sum_of(lax.rem(cell + n_cell - d, n_cell))]
        return remote(there, there, send_pair.at[d], recv_pair.at[d], member=mate)

    for d in range(1, n_cell):
        share_part(d).start()
        share_gain(d).start()
    for f, c in late_edges[LATE_FIRST:LATE_SECOND]:
        send_edges(f, c)
    for d in range(1, n_cell):
        share_part(d).wait_recv()
    summed = mine[part_of(cell), :]
    for d in range(n_cell - 1):
        summed = summed + others[d]
    gram[sum_of(cell), :] = summed
    for d in range(1, n_cell):
        share_sum(d).start()
    pair_sum(0).start()
    for f, c in late_edges[LATE_SECOND:]:
        send_edges(f, c)
    for f, c in late_edges[:LATE_SECOND]:
        wait_edges(f, c)
        stencil_chunk(f, c)
    for d in range(1, n_cell):
        share_sum(d).wait_recv()
        pair_sum(d).start()
    for f, c in late_edges[LATE_SECOND:]:
        wait_edges(f, c)
        stencil_chunk(f, c)
    for f in range(2, fields):
        for u in units_of[f]:
            send_far_unit(u)
    for d in range(n_cell):
        pair_sum(d).wait_recv()
    for f in range(fields):
        own_to_mate(f).start()

    lines = lax.broadcasted_iota(jnp.int32, (members, members), 0)
    columns = lax.broadcasted_iota(jnp.int32, (members, members), 1)
    identity = jnp.where(lines == columns, 1.0, 0.0).astype(jnp.float32)
    precision = gram[...] + (members - 1.0) * identity
    scale = jnp.sum(jnp.sum(precision * identity, axis=1, keepdims=True), axis=0, keepdims=True)
    upper[...] = precision / scale
    lower[...] = identity

    def newton(split, product, powers, of_root):
        def step(at, carry):
            x, z = upper[...], lower[...]
            pieces_of_x = split(x)
            square = product(pieces_of_x, pieces_of_x)
            lower[...] = of_root[0] * z + of_root[1] * three_products(split2(z), split2(x))
            cube = product(split(square), pieces_of_x)
            upper[...] = powers[0] * x + powers[1] * square + powers[2] * cube
            return carry

        return step

    growing, shrinking = (2.25, -1.5, 0.25), (0.0, 0.75, 0.25)
    exact, double = phase_ends(members, slots * n_cell)
    lax.fori_loop(0, exact, newton(split3, six_in_halves, growing, (1.5, -0.5)), 0)
    for u in units_of[0]:
        forward_unit(u)
    lax.fori_loop(exact, double, newton(split2, three_products, growing, (1.5, -0.5)), 0)
    for u in units_of[1]:
        forward_unit(u)
    upper[...] = identity - upper[...]
    lax.fori_loop(double, ROOT_STEPS, newton(split1, one_product, shrinking, (1.0, 0.5)), 0)

    for d in range(1, n_cell):
        share_gain(d).wait_recv()
    gain = gains[0]
    for d in range(1, n_cell):
        gain = gain + gains[d]
    gain = jnp.broadcast_to(gain, (8, members))
    root_pieces = split2(lower[...])
    half_way = three_products(split2(gain), root_pieces)
    mean_weights = three_products(split2(half_way), root_pieces)[0:1, :] / scale
    root = jnp.sqrt((members - 1.0) / scale) * lower[own, :]
    blend = mean_weights + root
    transform = blend - jnp.mean(blend, axis=1, keepdims=True) + 1.0 / members
    coeff[...] = transform.astype(jnp.bfloat16)

    def arrive(u):
        for d in range(1, chips):
            to_mate(d, u).wait_recv()

    def blend_row(f, r):
        block = pieces[:, f, r].reshape(members, width)
        out_ref[f, r] = jnp.dot(coeff[...], block, preferred_element_type=jnp.float32)

    own_to_mate(0).wait_recv()
    for u in units_of[0]:
        arrive(u)

    def blend_loop(r, carry):
        blend_row(0, r)
        return carry

    lax.fori_loop(0, rows, blend_loop, 0)
    own_to_mate(1).wait_recv()
    for u in units_of[1]:
        arrive(u)

    def blend_loop1(r, carry):
        blend_row(1, r)
        return carry

    lax.fori_loop(0, rows, blend_loop1, 0)
    for f in range(2, fields):
        own_to_mate(f).wait_recv()
    late = [u for f in range(2, fields) for u in units_of[f]]
    for at, u in enumerate(late):
        forward_unit(u)
        if at > 0:
            finish(arrive, blend_row, units, late[at - 1])
    finish(arrive, blend_row, units, late[-1])

    for f in range(fields):
        for c in range(chunks):

            @pl.when(has_north)
            def _():
                upward(f, c).wait_send()

            @pl.when(has_south)
            def _():
                downward(f, c).wait_send()

    for u in range(len(units)):
        for d in range(1, chips):
            to_far(d, u).wait_send()
            to_mate(d, u).wait_send()
    for f in range(fields):
        own_to_mate(f).wait_send()
    for d in range(1, chips):
        share_pred(d).wait_send()
    for d in range(chips):
        pass_pred(d).wait_send()
    for d in range(1, n_cell):
        share_part(d).wait_send()
        share_gain(d).wait_send()
        share_sum(d).wait_send()
    for d in range(n_cell):
        pair_sum(d).wait_send()


def row_cuts(f, fields, rows):
    if f < fields - 1:
        sizes = [rows // 2, rows // 2]
    else:
        sizes = [2] * (rows // 2 - 1) + [1, 1]
    return [(sum(sizes[:at]), size) for at, size in enumerate(sizes)]


def finish(arrive, blend_row, units, u):
    arrive(u)
    f, r, _ = units[u]
    for i in range(r.size):
        blend_row(f, r.start + i)


def write_kernel(blended_ref, out_hbm, sem):
    fields, rows = blended_ref.shape[:2]
    copies = [
        pltpu.make_async_copy(blended_ref.at[f, r], out_hbm.at[:, f, r, :], sem.at[f, r])
        for f in range(fields)
        for r in range(rows)
    ]
    for copy in copies:
        copy.start()
    for copy in copies:
        copy.wait()


def shards(prior_sample_set, wind_table, regimes, obs_index, obs_count, obs_value, obs_var):
    n_cell, n_member = lax.axis_size("cell"), lax.axis_size("member")
    count, fields, rows, width = prior_sample_set.shape
    slots = obs_index.shape[1]
    members = count * n_member
    chips = n_member // 2
    chunks = count // CHUNK
    units = chunks + sum(len(row_cuts(f, fields, rows)) for f in range(1, fields))
    vmem = pl.BlockSpec(memory_space=pltpu.VMEM)
    hbm = pl.BlockSpec(memory_space=pltpu.HBM)
    single, half = jnp.float32, jnp.bfloat16
    edge = pltpu.VMEM((fields, HALO, count, width), half)
    square = pltpu.VMEM((members, members), single)
    part = (members // 2 // n_cell, members)
    dma = pltpu.SemaphoreType.DMA
    operands = [regimes.T, wind_table.T, obs_index, obs_value, obs_var, prior_sample_set]
    operands = [pltpu.with_memory_space_constraint(x, pltpu.HBM) for x in operands]
    blended = pl.pallas_call(
        functools.partial(cycle_kernel, n_cell, n_member),
        in_specs=[pl.BlockSpec(memory_space=pltpu.SMEM)] + [hbm] * 6,
        out_specs=vmem,
        out_shape=jax.ShapeDtypeStruct((fields, rows, count, width), single),
        scratch_shapes=[
            pltpu.SMEM(operands[0].shape, jnp.int32),
            pltpu.SMEM(operands[1].shape, single),
            pltpu.VMEM(operands[2].shape, jnp.int32),
            pltpu.VMEM(operands[3].shape, single),
            pltpu.VMEM(operands[4].shape, single),
            pltpu.SMEM((SUBSTEPS * 5, rows + 2 * HALO), single),
            pltpu.VMEM((fields, rows, count, width), single),
            pltpu.VMEM((rows, width, slots), half),
            pltpu.VMEM((rows, count, width), single),
            edge,
            edge,
            edge,
            edge,
            pltpu.VMEM((n_member, fields, rows, count, width), half),
            pltpu.VMEM((count, members), half),
            pltpu.VMEM((members, slots), single),
            pltpu.VMEM((members, slots), single),
            pltpu.VMEM((members // 2, members), single),
            pltpu.VMEM((n_cell - 1,) + part, single),
            pltpu.VMEM((n_cell, 1, members), single),
            square,
            square,
            square,
            dma((fields, rows)),
            dma((5,)),
        ]
        + [dma((fields * chunks,))] * 4
        + [dma((chips,))] * 4
        + [dma((n_cell,))] * 8
        + [dma((chips, units))] * 4
        + [dma((fields,))] * 2,
        compiler_params=pltpu.CompilerParams(
            collective_id=0, has_side_effects=True, vmem_limit_bytes=VMEM_LIMIT
        ),
    )(obs_count, *operands)
    return pl.pallas_call(
        write_kernel,
        in_specs=[vmem],
        out_specs=hbm,
        out_shape=jax.ShapeDtypeStruct(prior_sample_set.shape, single),
        scratch_shapes=[dma((fields, rows))],
        compiler_params=pltpu.CompilerParams(vmem_limit_bytes=8 * 1024 * 1024),
    )(blended)


def solution(mesh):
    return jax.shard_map(
        shards,
        mesh=mesh,
        in_specs=(
            P(("groups", "member"), None, "cell", None),
            P(),
            P("groups", None),
            P(("groups", "cell"), None),
            P(("groups", "cell")),
            P(("groups", "cell"), None),
            P(("groups", "cell"), None),
        ),
        out_specs=P(("groups", "member"), None, "cell", None),
        check_vma=False,
    )
```
